32 devices in a mesh: dp: 2 (over x), context: 16 (over z, y, core).
Axes of the slice: x: 2, y: 2, z: 4, core: 2. Of those that a mesh axis runs over, the one named last changes fastest.
Arguments:
- grad_out: bfloat16 [2, 2048, 4096], P('dp', 'context'), may hold values from -6 to 6
- attn: bfloat16 [2, 2048, 4096], P('dp', 'context'), may hold values from -0.09375 to 0.09375
- w_out: bfloat16 [4096, 4096], P('context'), may hold values from -0.09375 to 0.09375
Outputs:
- grad_attn: bfloat16 [2, 2048, 4096], P('dp', None, 'context')
- grad_w: bfloat16 [4096, 4096], P('context')
The draws below stay inside these ranges and needn't reach their ends.
All inputs are finite; a program needn't handle non-finite values.
Results may differ from the reference program's by a relative error of at most 0.013.
Values may be sent and summed in bfloat16 or wider, within the bound.
A program may use at most 128 MiB of HBM per device.

```python
import jax
import jax.numpy as jnp
from jax import lax

D = 4096
HD = 4096
LEN = 2048
SEQS = 2


def shard_levels(key, shape, split, smallest, top_value):
    loudness, own = 1.0, jax.random.fold_in(key, 6)
    for dim, parts in split:
        heights = jnp.exp(jax.random.uniform(jax.random.fold_in(own, dim), (parts,), jnp.float32, smallest / len(split), top_value / len(split)))
        loudness = loudness * jnp.repeat(heights, shape[dim] // parts).reshape([-1 if axis == dim else 1 for axis in range(len(shape))])
    return loudness


def scatter_about(stream_key, shape, width, reach, split=(), kind=jnp.bfloat16):
    entries = width * jax.random.normal(stream_key, shape, jnp.float32)
    if split:
        entries = entries * shard_levels(stream_key, shape, split, -0.22, 0.18)
    return jnp.clip(entries, -reach, reach).astype(kind)


def setup_inputs(seed: int = 0) -> dict:
    seeds = jax.random.split(jax.random.key(seed), 4)
    grad_out = scatter_about(seeds[0], (SEQS, LEN, D), 1.0, 6.0, ((0, 2), (1, 16)))
    attn = scatter_about(seeds[1], (SEQS, LEN, HD), ((SEQS * LEN) ** -0.5), 0.09375, ((0, 2), (1, 16)))
    w_out = scatter_about(seeds[2], (HD, D), HD ** -0.5, 0.09375, ((0, 16),))
    return {"grad_out": grad_out, "attn": attn, "w_out": w_out}


def reference(grad_out, attn, w_out):
    def one_sequence(totals, inputs):
        cotangent, activations = inputs
        head_grad = jnp.dot(cotangent, w_out.T, preferred_element_type=jnp.float32).astype(jnp.bfloat16)
        partial_grad = jnp.dot(activations.T, cotangent, preferred_element_type=jnp.float32).astype(jnp.bfloat16)
        partial_grad = lax.optimization_barrier(partial_grad)
        return totals + partial_grad.astype(jnp.float32), head_grad

    start_totals = jnp.zeros((w_out.shape[0], w_out.shape[1]), jnp.float32)
    totals, head_grads = lax.scan(one_sequence, start_totals, (grad_out, attn))
    return head_grads, totals.astype(jnp.bfloat16)
```

```python
import functools

import jax
import jax.numpy as jnp
from jax import lax
from jax.experimental import pallas as pl
from jax.experimental.pallas import tpu as pltpu
from jax.sharding import PartitionSpec as P

CHUNKS = 8
AHEAD = 2
CORES = 2


def grid_of(chips):
    fast = 1
    while (2 * fast) * (2 * fast) <= chips:
        fast *= 2
    return chips // fast, fast


def kernel(dp, n, chunks, g_in, a_in, w_in, o_attn, o_w, gath, acts, acts_t, w, acc, part, stage_w, stage_a,
           g_send, g_recv, a_send, a_recv, x_send, x_recv, own_sem, w_sem, own_a_sem, ow_sem, oa_sem):
    A, B = grid_of(n // CORES)
    tokens, width = g_in.shape
    heads = w_in.shape[0]
    F = width // chunks
    me = lax.axis_index("context")
    rep = lax.axis_index("dp")
    c = lax.rem(me, CORES)
    b = lax.rem(me // CORES, B)
    a = me // (CORES * B)

    def ctx(a_, b_, c_):
        return (a_ * B + b_) * CORES + c_

    def others(i, size):
        return [lax.rem(i + d, size) for d in range(1, size)]

    def cols(k):
        return pl.ds(pl.multiple_of(k * F, F), F)

    def rows(j):
        return pl.ds(pl.multiple_of(j * tokens, tokens), tokens)

    def block(k, j):
        return gath.at[k, rows(j)]

    def move(src, k, j, target, slot):
        return pltpu.make_async_remote_copy(
            src_ref=src, dst_ref=block(k, j), send_sem=g_send.at[k, slot], recv_sem=g_recv.at[k, j],
            device_id={"context": target}, device_id_type=pl.DeviceIdType.MESH)

    def arrived(k, j):
        move(block(k, j), k, j, me, 0).wait_recv()

    barrier = pltpu.get_barrier_semaphore()
    for j in others(me, n):
        pl.semaphore_signal(barrier, inc=1, device_id={"context": j}, device_id_type=pl.DeviceIdType.MESH)
    for r in others(rep, dp):
        pl.semaphore_signal(barrier, inc=1, device_id={"dp": r}, device_id_type=pl.DeviceIdType.MESH)
    pl.semaphore_wait(barrier, n - 1 + dp - 1)

    Z0, RELAY, Y0 = 0, A - 1, A
    S0 = Y0 + A * (B - 1)

    def own(k):
        return g_in.at[:, cols(k)]

    def skip_far(target):
        end = jnp.logical_or(target == 0, target == A - 1)
        return jnp.logical_and(end, jnp.logical_or(target == a + 2, target == a - 2))

    def z_moves(k, act):
        for i, t in enumerate(others(a, A)):
            @pl.when(jnp.logical_not(skip_far(t)))
            def _():
                act(move(own(k), k, me, ctx(t, b, c), Z0 + i))

    def y_own_moves(k, act):
        for i, t in enumerate(others(b, B)):
            act(move(own(k), k, me, ctx(a, t, c), Y0 + i))

    def sib_own(k, act):
        act(move(own(k), k, me, ctx(a, b, 1 - c), S0))

    def relay_moves(k, act):
        @pl.when(a == 1)
        def _():
            j = ctx(2, b, c)
            act(move(block(k, j), k, j, ctx(0, b, c), RELAY))
        if A != 3:
            @pl.when(a == A - 2)
            def _():
                j = ctx(A - 3, b, c)
                act(move(block(k, j), k, j, ctx(A - 1, b, c), RELAY))

    def column_moves(k, s, t, act):
        j = ctx(t, b, c)
        for i, u in enumerate(others(b, B)):
            act(move(block(k, j), k, j, ctx(a, u, c), Y0 + (s + 1) * (B - 1) + i))
        act(move(block(k, j), k, j, ctx(a, b, 1 - c), S0 + 1 + s))

    def plane_moves(k, act, wait):
        slot = S0 + A
        for u in others(b, B):
            for d in range(A):
                j = ctx(lax.rem(a + d, A), u, c)
                if wait:
                    arrived(k, j)
                act(move(block(k, j), k, j, ctx(a, b, 1 - c), slot))
                slot += 1

    def own_copy(k):
        return pltpu.make_async_copy(own(k), block(k, me), own_sem.at[k])

    def w_copy(k):
        return pltpu.make_async_copy(w_in.at[:, cols(k)], w.at[k], w_sem.at[k])

    def head_cols(j):
        return pl.ds(pl.multiple_of(j * heads, heads), heads)

    def act_move(i, target):
        return pltpu.make_async_remote_copy(
            src_ref=a_in.at[:, head_cols(target)], dst_ref=acts.at[me], send_sem=a_send.at[i],
            recv_sem=a_recv.at[me], device_id={"context": target}, device_id_type=pl.DeviceIdType.MESH)

    own_act = pltpu.make_async_copy(a_in.at[:, head_cols(me)], acts.at[me], own_a_sem)

    def start(m):
        m.start()

    def done(m):
        m.wait_send()

    def x_moves(k, act):
        for i, r in enumerate(others(rep, dp)):
            act(pltpu.make_async_remote_copy(
                src_ref=part.at[rep, k], dst_ref=part.at[rep, k], send_sem=x_send.at[k, i],
                recv_sem=x_recv.at[k, rep], device_id={"dp": r}, device_id_type=pl.DeviceIdType.MESH))

    def x_arrived(k):
        for r in others(rep, dp):
            pltpu.make_async_remote_copy(
                src_ref=part.at[r, k], dst_ref=part.at[r, k], send_sem=x_send.at[k, 0],
                recv_sem=x_recv.at[k, r], device_id={"dp": rep}, device_id_type=pl.DeviceIdType.MESH).wait_recv()

    z_moves(0, start)
    targets = others(me, n)
    for i, t in enumerate(targets):
        act_move(i, t).start()
    own_act.start()

    @pl.loop(0, chunks)
    def _(k):
        y_own_moves(k, start)
        sib_own(k, start)
        own_copy(k).start()
        w_copy(k).start()

    for k in range(1, AHEAD):
        z_moves(k, start)

    def columns(k):
        for s, t in enumerate(others(a, A)):
            arrived(k, ctx(t, b, c))
            column_moves(k, s, t, start)
        relay_moves(k, start)

    row_tile = min(512, tokens * n)
    tiles = tokens * n // row_tile

    def out_attn(i):
        r = pl.ds(pl.multiple_of(i * row_tile, row_tile), row_tile)
        return pltpu.make_async_copy(stage_a.at[r], o_attn.at[r], oa_sem.at[i])

    def compute(k):
        own_copy(k).wait()
        w_copy(k).wait()
        for t in range(A):
            for u in range(B):
                arrived(k, ctx(t, u, 1 - c))

        @pl.when(k == 0)
        def _():
            own_act.wait()
            for t in targets:
                pltpu.make_async_remote_copy(
                    src_ref=acts.at[t], dst_ref=acts.at[t], send_sem=a_send.at[0], recv_sem=a_recv.at[t],
                    device_id={"context": me}, device_id_type=pl.DeviceIdType.MESH).wait_recv()
            for j in range(n):
                acts_t[:, j * tokens:(j + 1) * tokens] = acts[j].T
            acc[...] = jnp.zeros_like(acc)

        part[rep, k] = jnp.dot(acts_t[...], gath[k], preferred_element_type=jnp.float32).astype(part.dtype)
        x_moves(k, start)

        @pl.loop(0, tiles)
        def _(i):
            r = pl.ds(pl.multiple_of(i * row_tile, row_tile), row_tile)
            total = acc[r] + lax.dot_general(
                gath[k, r], w[k], (((1,), (1,)), ((), ())), preferred_element_type=jnp.float32)

            @pl.when(k < chunks - 1)
            def _():
                acc[r] = total

            @pl.when(k == chunks - 1)
            def _():
                stage_a[r] = total.astype(stage_a.dtype)
                out_attn(i).start()

    def out_w(k):
        return pltpu.make_async_copy(stage_w.at[k], o_w.at[:, cols(k)], ow_sem.at[k])

    def finish(k):
        x_arrived(k)
        total = part[0, k].astype(jnp.float32)
        for r in range(1, dp):
            total += part[r, k].astype(jnp.float32)
        stage_w[k] = total.astype(stage_w.dtype)
        out_w(k).start()

    @pl.loop(0, chunks + 2)
    def _(i):
        @pl.when(i + AHEAD < chunks)
        def _():
            z_moves(i + AHEAD, start)

        @pl.when(i < chunks)
        def _():
            columns(i)

        @pl.when(jnp.logical_and(i >= 1, i <= chunks))
        def _():
            plane_moves(i - 1, start, True)
            compute(i - 1)

        @pl.when(i >= 2)
        def _():
            finish(i - 2)

    @pl.loop(0, chunks)
    def _(k):
        z_moves(k, done)
        y_own_moves(k, done)
        sib_own(k, done)
        for s, t in enumerate(others(a, A)):
            column_moves(k, s, t, done)
        relay_moves(k, done)
        plane_moves(k, done, False)
        x_moves(k, done)
        out_w(k).wait()

    for i, t in enumerate(targets):
        act_move(i, t).wait_send()

    @pl.loop(0, tiles)
    def _(i):
        out_attn(i).wait()


def local(dp, n, grad_out, attn, w_out):
    g, x = grad_out[0], attn[0]
    tokens, width = g.shape
    heads = w_out.shape[0]
    length = tokens * n
    chunks = CHUNKS
    F = width // chunks
    A, B = grid_of(n // CORES)
    sends = A + A * (B - 1) + A * B
    tiles = length // min(512, length)
    any_ = pl.BlockSpec(memory_space=pl.ANY)
    bf = jnp.bfloat16
    dma = pltpu.SemaphoreType.DMA
    h, gw = pl.pallas_call(
        functools.partial(kernel, dp, n, chunks),
        out_shape=(jax.ShapeDtypeStruct((length, heads), bf), jax.ShapeDtypeStruct((heads, width), bf)),
        in_specs=[any_] * 3,
        out_specs=(any_, any_),
        scratch_shapes=[
            pltpu.VMEM((chunks, length, F), bf),
            pltpu.VMEM((n, tokens, heads), bf),
            pltpu.VMEM((heads, length), bf),
            pltpu.VMEM((chunks, heads, F), bf),
            pltpu.VMEM((length, heads), jnp.float32),
            pltpu.VMEM((dp, chunks, heads, F), bf),
            pltpu.VMEM((chunks, heads, F), bf),
            pltpu.VMEM((length, heads), bf),
            dma((chunks, sends)), dma((chunks, n)), dma((n - 1,)), dma((n,)),
            dma((chunks, dp - 1)), dma((chunks, dp)),
            dma((chunks,)), dma((chunks,)), dma, dma((chunks,)), dma((tiles,)),
        ],
        compiler_params=pltpu.CompilerParams(
            collective_id=0, has_side_effects=True, vmem_limit_bytes=62 * 2**20),
    )(g, x, w_out)
    return h[None], gw


def solution(mesh):
    dp, n = mesh.shape["dp"], mesh.shape["context"]
    in_specs = (P("dp", "context", None), P("dp", "context", None), P("context", None))
    out_specs = (P("dp", None, "context"), P("context", None))
    return jax.shard_map(functools.partial(local, dp, n), mesh=mesh, in_specs=in_specs, out_specs=out_specs,
                         check_vma=False)
```

```python
import functools

import jax
import jax.numpy as jnp
from jax import lax
from jax.experimental import pallas as pl
from jax.experimental.pallas import tpu as pltpu
from jax.sharding import PartitionSpec as P

CHUNKS = 16
AHEAD = 3
AHEAD_Y = 12
CORES = 2


def grid_of(chips):
    fast = 1
    while (2 * fast) * (2 * fast) <= chips:
        fast *= 2
    return chips // fast, fast


def kernel(dp, n, chunks, g_in, a_in, w_in, o_attn, o_w, gath, acts, acts_t, w, acc, part, stage_w, stage_a,
           g_send, g_recv, p_send, p_recv, a_send, a_recv, x_send, x_recv, own_sem, w_sem, own_a_sem, ow_sem, oa_sem):
    A, B = grid_of(n // CORES)
    tokens, width = g_in.shape
    heads = w_in.shape[0]
    F = width // chunks
    me = lax.axis_index("context")
    rep = lax.axis_index("dp")
    c = lax.rem(me, CORES)
    b = lax.rem(me // CORES, B)
    a = me // (CORES * B)

    def ctx(a_, b_, c_):
        return (a_ * B + b_) * CORES + c_

    def others(i, size):
        return [lax.rem(i + d, size) for d in range(1, size)]

    def cols(k):
        return pl.ds(pl.multiple_of(k * F, F), F)

    def rows(j):
        return pl.ds(pl.multiple_of(j * tokens, tokens), tokens)

    def block(k, j):
        return gath.at[k, rows(j)]

    def move(src, k, j, target, slot):
        return pltpu.make_async_remote_copy(
            src_ref=src, dst_ref=block(k, j), send_sem=g_send.at[k, slot], recv_sem=g_recv.at[k, j],
            device_id={"context": target}, device_id_type=pl.DeviceIdType.MESH)

    def arrived(k, j):
        move(block(k, j), k, j, me, 0).wait_recv()

    barrier = pltpu.get_barrier_semaphore()
    for j in others(me, n):
        pl.semaphore_signal(barrier, inc=1, device_id={"context": j}, device_id_type=pl.DeviceIdType.MESH)
    for r in others(rep, dp):
        pl.semaphore_signal(barrier, inc=1, device_id={"dp": r}, device_id_type=pl.DeviceIdType.MESH)
    pl.semaphore_wait(barrier, n - 1 + dp - 1)

    Z0, Y0 = 0, A + 1
    S0 = Y0 + A * (B - 1)
    pair = a + 1 - 2 * lax.rem(a, 2)
    side = 3 * tokens // 8

    def own(k):
        return g_in.at[:, cols(k)]

    def part_of(k, j, first):
        size = side if first else tokens - side
        lo = pl.multiple_of(j * tokens + (0 if first else side), 16)
        return gath.at[k, pl.ds(lo, size)]

    def inside(t):
        return jnp.logical_and(t >= 0, t < A)

    def z_moves(k, act):
        for sign, slot in ((1, Z0 + a), (-1, Z0 + A)):
            @pl.when(inside(a + sign))
            def _():
                act(move(own(k), k, me, ctx(a + sign, b, c), slot))

    def y_own_moves(k, act):
        for i, t in enumerate(others(b, B)):
            act(move(own(k), k, me, ctx(a, t, c), Y0 + a * (B - 1) + i))

    def sib_own(k, act):
        act(move(own(k), k, me, ctx(a, b, 1 - c), S0 + a))

    def rest_move(k, j, target, slot):
        return pltpu.make_async_remote_copy(
            src_ref=part_of(k, j, False), dst_ref=part_of(k, j, False), send_sem=g_send.at[k, slot],
            recv_sem=g_recv.at[k, j], device_id={"context": target}, device_id_type=pl.DeviceIdType.MESH)

    def side_move(k, j, target, i):
        return pltpu.make_async_remote_copy(
            src_ref=part_of(k, j, True), dst_ref=part_of(k, j, True), send_sem=p_send.at[k, i],
            recv_sem=p_recv.at[k, j], device_id={"context": target}, device_id_type=pl.DeviceIdType.MESH)

    def side_moves(k, act, wait):
        for i, u in enumerate(others(b, B)):
            j = ctx(a, u, c)
            if wait:
                arrived(k, j)
            act(side_move(k, j, ctx(pair, b, c), i))
            act(move(block(k, j), k, j, ctx(a, b, 1 - c), S0 + A * (1 + i) + a))

    def column_moves(k, d, act, wait):
        for sign in (1, -1):
            t = a + sign * d

            @pl.when(inside(t))
            def _():
                j = ctx(t, b, c)
                if wait:
                    arrived(k, j)

                @pl.when(inside(a - sign))
                def _():
                    act(move(block(k, j), k, j, ctx(a - sign, b, c), Z0 + t))
                for i, u in enumerate(others(b, B)):
                    slot = Y0 + t * (B - 1) + i
                    if d > 1:
                        act(move(block(k, j), k, j, ctx(a, u, c), slot))
                    else:
                        @pl.when(t == pair)
                        def _():
                            act(rest_move(k, j, ctx(a, u, c), slot))

                        @pl.when(t != pair)
                        def _():
                            act(move(block(k, j), k, j, ctx(a, u, c), slot))
                act(move(block(k, j), k, j, ctx(a, b, 1 - c), S0 + t))

    def plane_moves(k, act, wait):
        for i, u in enumerate(others(b, B)):
            for d in range(1, A):
                t = lax.rem(a + d, A)
                j = ctx(t, u, c)
                if wait:
                    @pl.when(t == pair)
                    def _():
                        rest_move(k, j, me, 0).wait_recv()
                        side_move(k, j, me, 0).wait_recv()

                    @pl.when(t != pair)
                    def _():
                        arrived(k, j)
                act(move(block(k, j), k, j, ctx(a, b, 1 - c), S0 + A * (1 + i) + t))

    def own_copy(k):
        return pltpu.make_async_copy(own(k), block(k, me), own_sem.at[k])

    def w_copy(k):
        return pltpu.make_async_copy(w_in.at[:, cols(k)], w.at[k], w_sem.at[k])

    def head_cols(j):
        return pl.ds(pl.multiple_of(j * heads, heads), heads)

    def act_move(i, target):
        return pltpu.make_async_remote_copy(
            src_ref=a_in.at[:, head_cols(target)], dst_ref=acts.at[me], send_sem=a_send.at[i],
            recv_sem=a_recv.at[me], device_id={"context": target}, device_id_type=pl.DeviceIdType.MESH)

    own_act = pltpu.make_async_copy(a_in.at[:, head_cols(me)], acts.at[me], own_a_sem)

    def start(m):
        m.start()

    def done(m):
        m.wait_send()

    def x_moves(k, act):
        for i, r in enumerate(others(rep, dp)):
            act(pltpu.make_async_remote_copy(
                src_ref=part.at[rep, k], dst_ref=part.at[rep, k], send_sem=x_send.at[k, i],
                recv_sem=x_recv.at[k, rep], device_id={"dp": r}, device_id_type=pl.DeviceIdType.MESH))

    def x_arrived(k):
        for r in others(rep, dp):
            pltpu.make_async_remote_copy(
                src_ref=part.at[r, k], dst_ref=part.at[r, k], send_sem=x_send.at[k, 0],
                recv_sem=x_recv.at[k, r], device_id={"dp": rep}, device_id_type=pl.DeviceIdType.MESH).wait_recv()

    for k in range(AHEAD):
        z_moves(k, start)
    targets = others(me, n)
    for i, t in enumerate(targets):
        act_move(i, t).start()
    own_act.start()

    for k in range(AHEAD_Y):
        y_own_moves(k, start)
        sib_own(k, start)

    @pl.loop(0, chunks)
    def _(k):
        own_copy(k).start()
        w_copy(k).start()

    row_tile = min(512, tokens * n)
    tiles = tokens * n // row_tile

    def out_attn(i):
        r = pl.ds(pl.multiple_of(i * row_tile, row_tile), row_tile)
        return pltpu.make_async_copy(stage_a.at[r], o_attn.at[r], oa_sem.at[i])

    def compute(k):
        own_copy(k).wait()
        w_copy(k).wait()
        for t in range(A):
            for u in range(B):
                arrived(k, ctx(t, u, 1 - c))

        @pl.when(k == 0)
        def _():
            own_act.wait()
            for t in targets:
                pltpu.make_async_remote_copy(
                    src_ref=acts.at[t], dst_ref=acts.at[t], send_sem=a_send.at[0], recv_sem=a_recv.at[t],
                    device_id={"context": me}, device_id_type=pl.DeviceIdType.MESH).wait_recv()
            for j in range(n):
                acts_t[:, j * tokens:(j + 1) * tokens] = acts[j].T
            acc[...] = jnp.zeros_like(acc)

        part[rep, k] = jnp.dot(acts_t[...], gath[k], preferred_element_type=jnp.float32).astype(part.dtype)
        x_moves(k, start)

        @pl.loop(0, tiles)
        def _(i):
            r = pl.ds(pl.multiple_of(i * row_tile, row_tile), row_tile)
            total = acc[r] + lax.dot_general(
                gath[k, r], w[k], (((1,), (1,)), ((), ())), preferred_element_type=jnp.float32)

            @pl.when(k < chunks - 1)
            def _():
                acc[r] = total

            @pl.when(k == chunks - 1)
            def _():
                stage_a[r] = total.astype(stage_a.dtype)
                out_attn(i).start()

    def out_w(k):
        return pltpu.make_async_copy(stage_w.at[k], o_w.at[:, cols(k)], ow_sem.at[k])

    def finish(k):
        x_arrived(k)
        total = part[0, k].astype(jnp.float32)
        for r in range(1, dp):
            total += part[r, k].astype(jnp.float32)
        stage_w[k] = total.astype(stage_w.dtype)
        out_w(k).start()

    def stage(k, f):
        pl.when(jnp.logical_and(k >= 0, k < chunks))(functools.partial(f, k))

    @pl.loop(0, chunks + A + 2)
    def _(i):
        def ahead_z(k):
            z_moves(k, start)

        def ahead_y(k):
            y_own_moves(k, start)
            sib_own(k, start)

        stage(i + AHEAD, ahead_z)
        stage(i + AHEAD_Y, ahead_y)
        for d in range(1, A):
            stage(i - d + 1, lambda k, d=d: column_moves(k, d, start, True))
            if d == 1:
                stage(i, lambda k: side_moves(k, start, True))
        stage(i - A + 1, lambda k: plane_moves(k, start, True))
        stage(i - A, compute)
        stage(i - A - 1, finish)

    @pl.loop(0, chunks)
    def _(k):
        z_moves(k, done)
        y_own_moves(k, done)
        sib_own(k, done)
        side_moves(k, done, False)
        for d in range(1, A):
            column_moves(k, d, done, False)
        plane_moves(k, done, False)
        x_moves(k, done)
        out_w(k).wait()

    for i, t in enumerate(targets):
        act_move(i, t).wait_send()

    @pl.loop(0, tiles)
    def _(i):
        out_attn(i).wait()


def local(dp, n, grad_out, attn, w_out):
    g, x = grad_out[0], attn[0]
    tokens, width = g.shape
    heads = w_out.shape[0]
    length = tokens * n
    chunks = CHUNKS
    F = width // chunks
    A, B = grid_of(n // CORES)
    sends = A + 1 + A * (B - 1) + A * B
    tiles = length // min(512, length)
    any_ = pl.BlockSpec(memory_space=pl.ANY)
    bf = jnp.bfloat16
    dma = pltpu.SemaphoreType.DMA
    h, gw = pl.pallas_call(
        functools.partial(kernel, dp, n, chunks),
        out_shape=(jax.ShapeDtypeStruct((length, heads), bf), jax.ShapeDtypeStruct((heads, width), bf)),
        in_specs=[any_] * 3,
        out_specs=(any_, any_),
        scratch_shapes=[
            pltpu.VMEM((chunks, length, F), bf),
            pltpu.VMEM((n, tokens, heads), bf),
            pltpu.VMEM((heads, length), bf),
            pltpu.VMEM((chunks, heads, F), bf),
            pltpu.VMEM((length, heads), jnp.float32),
            pltpu.VMEM((dp, chunks, heads, F), bf),
            pltpu.VMEM((chunks, heads, F), bf),
            pltpu.VMEM((length, heads), bf),
            dma((chunks, sends)), dma((chunks, n)), dma((chunks, B - 1)), dma((chunks, n)),
            dma((n - 1,)), dma((n,)),
            dma((chunks, dp - 1)), dma((chunks, dp)),
            dma((chunks,)), dma((chunks,)), dma, dma((chunks,)), dma((tiles,)),
        ],
        compiler_params=pltpu.CompilerParams(
            collective_id=0, has_side_effects=True, vmem_limit_bytes=62 * 2**20),
    )(g, x, w_out)
    return h[None], gw


def solution(mesh):
    dp, n = mesh.shape["dp"], mesh.shape["context"]
    in_specs = (P("dp", "context", None), P("dp", "context", None), P("context", None))
    out_specs = (P("dp", None, "context"), P("context", None))
    return jax.shard_map(functools.partial(local, dp, n), mesh=mesh, in_specs=in_specs, out_specs=out_specs,
                         check_vma=False)
```

```python
import functools

import jax
import jax.numpy as jnp
from jax import lax
from jax.experimental import pallas as pl
from jax.experimental.pallas import tpu as pltpu
from jax.sharding import PartitionSpec as P

CHUNKS = 16
AHEAD = 2
AHEAD_Y = 8
CORES = 2


def grid_of(chips):
    fast = 1
    while (2 * fast) * (2 * fast) <= chips:
        fast *= 2
    return chips // fast, fast


def kernel(dp, n, chunks, g_in, a_in, w_in, o_attn, o_w, gath, acts, acts_t, w, acc, part, stage_w, stage_a,
           g_send, g_recv, p_send, p_recv, a_send, a_recv, x_send, x_recv, own_sem, w_sem, own_a_sem, ow_sem, oa_sem):
    A, B = grid_of(n // CORES)
    tokens, width = g_in.shape
    heads = w_in.shape[0]
    F = width // chunks
    me = lax.axis_index("context")
    rep = lax.axis_index("dp")
    c = lax.rem(me, CORES)
    b = lax.rem(me // CORES, B)
    a = me // (CORES * B)

    def ctx(a_, b_, c_):
        return (a_ * B + b_) * CORES + c_

    def others(i, size):
        return [lax.rem(i + d, size) for d in range(1, size)]

    def cols(k):
        return pl.ds(pl.multiple_of(k * F, F), F)

    def rows(j):
        return pl.ds(pl.multiple_of(j * tokens, tokens), tokens)

    def block(k, j):
        return gath.at[k, rows(j)]

    def move(src, k, j, target, slot):
        return pltpu.make_async_remote_copy(
            src_ref=src, dst_ref=block(k, j), send_sem=g_send.at[k, slot], recv_sem=g_recv.at[k, j],
            device_id={"context": target}, device_id_type=pl.DeviceIdType.MESH)

    def arrived(k, j):
        move(block(k, j), k, j, me, 0).wait_recv()

    barrier = pltpu.get_barrier_semaphore()
    for j in others(me, n):
        pl.semaphore_signal(barrier, inc=1, device_id={"context": j}, device_id_type=pl.DeviceIdType.MESH)
    for r in others(rep, dp):
        pl.semaphore_signal(barrier, inc=1, device_id={"dp": r}, device_id_type=pl.DeviceIdType.MESH)
    pl.semaphore_wait(barrier, n - 1 + dp - 1)

    Z0, Y0 = 0, A + 1
    S0 = Y0 + A * (B - 1)
    pair = a + 1 - 2 * lax.rem(a, 2)
    side = tokens // 4

    def own(k):
        return g_in.at[:, cols(k)]

    def part_of(k, j, first):
        size = side if first else tokens - side
        lo = pl.multiple_of(j * tokens + (0 if first else side), 16)
        return gath.at[k, pl.ds(lo, size)]

    def inside(t):
        return jnp.logical_and(t >= 0, t < A)

    def z_moves(k, act):
        for sign, slot in ((1, Z0 + a), (-1, Z0 + A)):
            @pl.when(inside(a + sign))
            def _():
                act(move(own(k), k, me, ctx(a + sign, b, c), slot))

    def y_own_moves(k, act):
        for i, t in enumerate(others(b, B)):
            act(move(own(k), k, me, ctx(a, t, c), Y0 + a * (B - 1) + i))

    def sib_own(k, act):
        act(move(own(k), k, me, ctx(a, b, 1 - c), S0 + a))

    def rest_move(k, j, target, slot):
        return pltpu.make_async_remote_copy(
            src_ref=part_of(k, j, False), dst_ref=part_of(k, j, False), send_sem=g_send.at[k, slot],
            recv_sem=g_recv.at[k, j], device_id={"context": target}, device_id_type=pl.DeviceIdType.MESH)

    def side_move(k, j, target, i):
        return pltpu.make_async_remote_copy(
            src_ref=part_of(k, j, True), dst_ref=part_of(k, j, True), send_sem=p_send.at[k, i],
            recv_sem=p_recv.at[k, j], device_id={"context": target}, device_id_type=pl.DeviceIdType.MESH)

    def side_moves(k, act, wait):
        for i, u in enumerate(others(b, B)):
            j = ctx(a, u, c)
            if wait:
                arrived(k, j)
            act(side_move(k, j, ctx(pair, b, c), i))
            act(move(block(k, j), k, j, ctx(a, b, 1 - c), S0 + A * (1 + i) + a))

    def column_moves(k, d, act, wait):
        for sign in (1, -1):
            t = a + sign * d

            @pl.when(inside(t))
            def _():
                j = ctx(t, b, c)
                if wait:
                    arrived(k, j)

                @pl.when(inside(a - sign))
                def _():
                    act(move(block(k, j), k, j, ctx(a - sign, b, c), Z0 + t))
                for i, u in enumerate(others(b, B)):
                    slot = Y0 + t * (B - 1) + i
                    if d > 1:
                        act(move(block(k, j), k, j, ctx(a, u, c), slot))
                    else:
                        @pl.when(t == pair)
                        def _():
                            act(rest_move(k, j, ctx(a, u, c), slot))

                        @pl.when(t != pair)
                        def _():
                            act(move(block(k, j), k, j, ctx(a, u, c), slot))
                act(move(block(k, j), k, j, ctx(a, b, 1 - c), S0 + t))

    def plane_moves(k, act, wait):
        for i, u in enumerate(others(b, B)):
            for d in range(1, A):
                t = lax.rem(a + d, A)
                j = ctx(t, u, c)
                if wait:
                    @pl.when(t == pair)
                    def _():
                        rest_move(k, j, me, 0).wait_recv()
                        side_move(k, j, me, 0).wait_recv()

                    @pl.when(t != pair)
                    def _():
                        arrived(k, j)
                act(move(block(k, j), k, j, ctx(a, b, 1 - c), S0 + A * (1 + i) + t))

    def own_copy(k):
        return pltpu.make_async_copy(own(k), block(k, me), own_sem.at[k])

    def w_copy(k):
        return pltpu.make_async_copy(w_in.at[:, cols(k)], w.at[k], w_sem.at[k])

    def head_cols(j):
        return pl.ds(pl.multiple_of(j * heads, heads), heads)

    def act_move(i, target):
        return pltpu.make_async_remote_copy(
            src_ref=a_in.at[:, head_cols(target)], dst_ref=acts.at[me], send_sem=a_send.at[i],
            recv_sem=a_recv.at[me], device_id={"context": target}, device_id_type=pl.DeviceIdType.MESH)

    own_act = pltpu.make_async_copy(a_in.at[:, head_cols(me)], acts.at[me], own_a_sem)

    def start(m):
        m.start()

    def done(m):
        m.wait_send()

    def x_moves(k, act):
        for i, r in enumerate(others(rep, dp)):
            act(pltpu.make_async_remote_copy(
                src_ref=part.at[rep, k], dst_ref=part.at[rep, k], send_sem=x_send.at[k, i],
                recv_sem=x_recv.at[k, rep], device_id={"dp": r}, device_id_type=pl.DeviceIdType.MESH))

    def x_arrived(k):
        for r in others(rep, dp):
            pltpu.make_async_remote_copy(
                src_ref=part.at[r, k], dst_ref=part.at[r, k], send_sem=x_send.at[k, 0],
                recv_sem=x_recv.at[k, r], device_id={"dp": rep}, device_id_type=pl.DeviceIdType.MESH).wait_recv()

    for k in range(AHEAD):
        z_moves(k, start)
    targets = others(me, n)
    for i, t in enumerate(targets):
        act_move(i, t).start()
    own_act.start()

    for k in range(AHEAD_Y):
        y_own_moves(k, start)
        sib_own(k, start)

    @pl.loop(0, chunks)
    def _(k):
        own_copy(k).start()
        w_copy(k).start()

    row_tile = min(512, tokens * n)
    tiles = tokens * n // row_tile

    def out_attn(i):
        r = pl.ds(pl.multiple_of(i * row_tile, row_tile), row_tile)
        return pltpu.make_async_copy(stage_a.at[r], o_attn.at[r], oa_sem.at[i])

    def compute(k):
        own_copy(k).wait()
        w_copy(k).wait()
        for t in range(A):
            for u in range(B):
                arrived(k, ctx(t, u, 1 - c))

        @pl.when(k == 0)
        def _():
            own_act.wait()
            for t in targets:
                pltpu.make_async_remote_copy(
                    src_ref=acts.at[t], dst_ref=acts.at[t], send_sem=a_send.at[0], recv_sem=a_recv.at[t],
                    device_id={"context": me}, device_id_type=pl.DeviceIdType.MESH).wait_recv()
            for j in range(n):
                acts_t[:, j * tokens:(j + 1) * tokens] = acts[j].T
            acc[...] = jnp.zeros_like(acc)

        part[rep, k] = jnp.dot(acts_t[...], gath[k], preferred_element_type=jnp.float32).astype(part.dtype)
        x_moves(k, start)

        @pl.loop(0, tiles)
        def _(i):
            r = pl.ds(pl.multiple_of(i * row_tile, row_tile), row_tile)
            total = acc[r] + lax.dot_general(
                gath[k, r], w[k], (((1,), (1,)), ((), ())), preferred_element_type=jnp.float32)

            @pl.when(k < chunks - 1)
            def _():
                acc[r] = total

            @pl.when(k == chunks - 1)
            def _():
                stage_a[r] = total.astype(stage_a.dtype)
                out_attn(i).start()

    def out_w(k):
        return pltpu.make_async_copy(stage_w.at[k], o_w.at[:, cols(k)], ow_sem.at[k])

    def finish(k):
        x_arrived(k)
        total = part[0, k].astype(jnp.float32)
        for r in range(1, dp):
            total += part[r, k].astype(jnp.float32)
        stage_w[k] = total.astype(stage_w.dtype)
        out_w(k).start()

    def stage(k, f):
        pl.when(jnp.logical_and(k >= 0, k < chunks))(functools.partial(f, k))

    @pl.loop(0, chunks + A + 2)
    def _(i):
        def ahead_z(k):
            z_moves(k, start)

        def ahead_y(k):
            y_own_moves(k, start)
            sib_own(k, start)

        stage(i + AHEAD, ahead_z)
        stage(i + AHEAD_Y, ahead_y)
        for d in range(1, A):
            stage(i - d + 1, lambda k, d=d: column_moves(k, d, start, True))
            if d == 1:
                stage(i, lambda k: side_moves(k, start, True))
        stage(i - A + 1, lambda k: plane_moves(k, start, True))
        stage(i - A, compute)
        stage(i - A - 1, finish)

    @pl.loop(0, chunks)
    def _(k):
        z_moves(k, done)
        y_own_moves(k, done)
        sib_own(k, done)
        side_moves(k, done, False)
        for d in range(1, A):
            column_moves(k, d, done, False)
        plane_moves(k, done, False)
        x_moves(k, done)
        out_w(k).wait()

    for i, t in enumerate(targets):
        act_move(i, t).wait_send()

    @pl.loop(0, tiles)
    def _(i):
        out_attn(i).wait()


def local(dp, n, grad_out, attn, w_out):
    g, x = grad_out[0], attn[0]
    tokens, width = g.shape
    heads = w_out.shape[0]
    length = tokens * n
    chunks = CHUNKS
    F = width // chunks
    A, B = grid_of(n // CORES)
    sends = A + 1 + A * (B - 1) + A * B
    tiles = length // min(512, length)
    any_ = pl.BlockSpec(memory_space=pl.ANY)
    bf = jnp.bfloat16
    dma = pltpu.SemaphoreType.DMA
    h, gw = pl.pallas_call(
        functools.partial(kernel, dp, n, chunks),
        out_shape=(jax.ShapeDtypeStruct((length, heads), bf), jax.ShapeDtypeStruct((heads, width), bf)),
        in_specs=[any_] * 3,
        out_specs=(any_, any_),
        scratch_shapes=[
            pltpu.VMEM((chunks, length, F), bf),
            pltpu.VMEM((n, tokens, heads), bf),
            pltpu.VMEM((heads, length), bf),
            pltpu.VMEM((chunks, heads, F), bf),
            pltpu.VMEM((length, heads), jnp.float32),
            pltpu.VMEM((dp, chunks, heads, F), bf),
            pltpu.VMEM((chunks, heads, F), bf),
            pltpu.VMEM((length, heads), bf),
            dma((chunks, sends)), dma((chunks, n)), dma((chunks, B - 1)), dma((chunks, n)),
            dma((n - 1,)), dma((n,)),
            dma((chunks, dp - 1)), dma((chunks, dp)),
            dma((chunks,)), dma((chunks,)), dma, dma((chunks,)), dma((tiles,)),
        ],
        compiler_params=pltpu.CompilerParams(
            collective_id=0, has_side_effects=True, vmem_limit_bytes=52 * 2**20),
    )(g, x, w_out)
    return h[None], gw


def solution(mesh):
    dp, n = mesh.shape["dp"], mesh.shape["context"]
    in_specs = (P("dp", "context", None), P("dp", "context", None), P("context", None))
    out_specs = (P("dp", None, "context"), P("context", None))
    return jax.shard_map(functools.partial(local, dp, n), mesh=mesh, in_specs=in_specs, out_specs=out_specs,
                         check_vma=False)
```
